128 devices in a mesh: row: 8 (over x_hi, y), col: 16 (over z, x_lo, core).
Axes of the slice: x: 4 (x_hi: 2, x_lo: 2; x = x_hi * 2 + x_lo), y: 4, z: 4, core: 2. Of those that a mesh axis runs over, the one named last changes fastest.
Arguments:
- user_emb: bfloat16 [32768, 256], P(('row', 'col')), may hold values from -8 to 8
- item_emb: bfloat16 [32768, 256], P(('row', 'col')), may hold values from -8 to 8
- user_cot: bfloat16 [32768, 256], P(('row', 'col')), may hold values from -8 to 8
- item_cot: bfloat16 [32768, 256], P(('row', 'col')), may hold values from -8 to 8
- tiles: bfloat16 [32768, 20480], P('row', 'col'), may hold values from 0 to 1, as said below
- tile_cols: int32 [256, 160], P('row', 'col'), may hold values from 0 to 15, as said below
- row_count: int32 [256, 16], P('row', 'col'), may hold values from 1 to 10, as said below
- user_deg: int32 [32768], P(('row', 'col')), may hold values from 21 to 81
- item_deg: int32 [32768], P(('row', 'col')), may hold values from 21 to 81
Outputs:
- user_next: float32 [32768, 256], P(('row', 'col'))
- item_next: float32 [32768, 256], P(('row', 'col'))
- user_grad: float32 [32768, 256], P(('row', 'col'))
- item_grad: float32 [32768, 256], P(('row', 'col'))
The draws below stay inside these ranges and needn't reach their ends.
Inputs may be any that keep to these rules, and one draw needn't show every extreme that they name: `tiles`: every entry is 0 or 1. `tile_cols`: within one block row of one device, the 10 slots name distinct item blocks; slots at or beyond row_count are unused. `row_count`: in every draw some block row of some device holds 10 tiles.
All inputs are finite; a program needn't handle non-finite values.
Results may differ from the reference program's by a relative error of at most 0.0029.
Values may be sent and summed in bfloat16 or wider, within the bound.
A program may use at most 128 MiB of HBM per device.

```python
import jax
import jax.numpy as jnp
from jax import lax

FEAT = 256
BLK = 128
UD = 256
ID = 256
GRID_ROWS = 8
GRID_COLS = 16
USERS = 32768
ITEMS = 32768
UBLK = 32
IBLK = 16
KR = 10
N_ROW = 8
N_COL = 16


def node_features(key, salt, count):
    salted = jax.random.fold_in(key, salt)
    values = jax.random.normal(jax.random.fold_in(salted, 2), (count, FEAT), jnp.float32)
    return jnp.clip(values, -8.0, 8.0).astype(jnp.bfloat16)


def draw_user_emb(key, part):
    return node_features(key, 11, USERS)


def draw_item_emb(key, part):
    return node_features(key, 12, ITEMS)


def draw_user_cot(key, part):
    return node_features(key, 13, USERS)


def draw_item_cot(key, part):
    return node_features(key, 14, ITEMS)


def draw_tiles(key, part):
    tile_rows = N_ROW * UBLK
    tile_slots = N_COL * KR
    levels = jax.random.randint(jax.random.fold_in(key, 31), (tile_rows, 1, tile_slots, 1), 2, 9)
    coin_flip = jax.random.randint(jax.random.fold_in(key, 32), (tile_rows, BLK, tile_slots, BLK), 0, 16)
    filled = (coin_flip < levels).astype(jnp.float32)
    return filled.reshape(tile_rows * BLK, tile_slots * BLK).astype(jnp.bfloat16)


def draw_tile_cols(key, part):
    scores = jax.random.randint(jax.random.fold_in(key, 51), (N_ROW * UBLK, N_COL, IBLK), 0, 65536)
    scores = scores * IBLK + jnp.arange(IBLK, dtype=jnp.int32)
    ranked = jnp.argsort(scores, axis=-1, stable=True).astype(jnp.int32)
    return ranked[:, :, :KR].reshape(N_ROW * UBLK, N_COL * KR)


def draw_row_count(key, part):
    heavy_device = jax.random.randint(jax.random.fold_in(key, 41), (N_ROW, 1, N_COL), 0, 4)
    weight = jnp.where(heavy_device == 3, 4, 1)
    uniform_part = jax.random.randint(jax.random.fold_in(key, 42), (N_ROW, UBLK, N_COL), 0, KR)
    counts = jnp.minimum(KR, 1 + uniform_part * weight // 4)
    special = jax.random.randint(jax.random.fold_in(key, 43), (), 0, N_ROW * UBLK * N_COL)
    places = jnp.arange(N_ROW * UBLK * N_COL, dtype=jnp.int32).reshape(N_ROW, UBLK, N_COL)
    counts = jnp.where(places == special, KR, counts)
    return counts.reshape(N_ROW * UBLK, N_COL).astype(jnp.int32)


def touch_ends(array, stream_key, low, top_value):
    extent = array.shape
    spot = [jax.random.randint(jax.random.fold_in(stream_key, axis), (), 0, extent[axis]) for axis in range(len(extent))]
    array = array.at[tuple(spot)].set(low)
    longest = extent.index(max(extent))
    spot[longest] = (spot[longest] + 1) % extent[longest]
    return array.at[tuple(spot)].set(top_value)


def setup_inputs(seed: int = 0) -> dict:
    arg_keys = jax.random.split(jax.random.key(seed), 10)
    user_emb = draw_user_emb(jax.random.fold_in(arg_keys[9], 71), 0)
    item_emb = draw_item_emb(jax.random.fold_in(arg_keys[9], 71), 0)
    user_cot = draw_user_cot(jax.random.fold_in(arg_keys[9], 71), 0)
    item_cot = draw_item_cot(jax.random.fold_in(arg_keys[9], 71), 0)
    tiles = draw_tiles(jax.random.fold_in(arg_keys[9], 71), 0)
    tile_cols = draw_tile_cols(jax.random.fold_in(arg_keys[9], 71), 0)
    row_count = draw_row_count(jax.random.fold_in(arg_keys[9], 71), 0)
    user_deg = touch_ends(jax.random.randint(arg_keys[7], (USERS,), GRID_COLS * KR * BLK // 1024 + 1, GRID_COLS * KR * BLK // 256 + 2), jax.random.fold_in(arg_keys[7], 1), GRID_COLS * KR * BLK // 1024 + 1, (GRID_COLS * KR * BLK // 256 + 2) - 1).astype(jnp.int32)
    item_deg = touch_ends(jax.random.randint(arg_keys[8], (ITEMS,), GRID_ROWS * UBLK * KR * BLK // (1024 * IBLK) + 1, GRID_ROWS * UBLK * KR * BLK // (256 * IBLK) + 2), jax.random.fold_in(arg_keys[8], 1), GRID_ROWS * UBLK * KR * BLK // (1024 * IBLK) + 1, (GRID_ROWS * UBLK * KR * BLK // (256 * IBLK) + 2) - 1).astype(jnp.int32)
    return {"user_emb": user_emb, "item_emb": item_emb, "user_cot": user_cot, "item_cot": item_cot, "tiles": tiles, "tile_cols": tile_cols, "row_count": row_count, "user_deg": user_deg, "item_deg": item_deg}


def scaled_side(former, latter, inverse_root):
    joined = jnp.concatenate([former, latter], axis=1).astype(jnp.float32)
    return (joined * inverse_root[:, None]).astype(jnp.bfloat16)

def reference(user_emb, item_emb, user_cot, item_cot, tiles, tile_cols, row_count, user_deg, item_deg):
    doubled = 2 * FEAT
    panel_users = N_COL * UD
    user_root = 1.0 / jnp.sqrt(user_deg.astype(jnp.float32))
    item_root = 1.0 / jnp.sqrt(item_deg.astype(jnp.float32))
    user_side = scaled_side(user_emb, user_cot, user_root)
    item_side = scaled_side(item_emb, item_cot, item_root)
    item_grid = item_side.reshape(N_ROW, N_COL, ID, doubled)

    def visit_device(device_id, totals):
        user_total, item_total = totals
        grid_row = (device_id // N_COL).astype(jnp.int32)
        grid_col = (device_id % N_COL).astype(jnp.int32)
        tile_part = lax.dynamic_slice(tiles, (grid_row * (UBLK * BLK), grid_col * (KR * BLK)), (UBLK * BLK, KR * BLK))
        col_ids = lax.dynamic_slice(tile_cols, (grid_row * UBLK, grid_col * KR), (UBLK, KR)).astype(jnp.int32)
        counts = lax.dynamic_slice(row_count, (grid_row * UBLK, grid_col), (UBLK, 1))
        live_mask = (jnp.arange(KR, dtype=jnp.int32)[None, :] < counts).astype(jnp.float32)
        tile_grid = tile_part.reshape(UBLK, BLK, KR, BLK).astype(jnp.float32) * live_mask[:, None, :, None]
        item_panel = lax.dynamic_slice_in_dim(item_grid, grid_col, 1, 1).reshape(IBLK, BLK, doubled).astype(jnp.float32)
        user_panel = lax.dynamic_slice_in_dim(user_side, grid_row * panel_users, panel_users, 0).reshape(UBLK, BLK, doubled).astype(jnp.float32)
        user_part = jnp.einsum('bikj,bkjf->bif', tile_grid, item_panel[col_ids])
        item_terms = jnp.einsum('bikj,bif->bkjf', tile_grid, user_panel).reshape(UBLK * KR, BLK, doubled)
        item_part = jax.ops.segment_sum(item_terms, col_ids.reshape(-1), num_segments=IBLK)
        old_users = lax.dynamic_slice_in_dim(user_total, grid_row * panel_users, panel_users, 0)
        user_total = lax.dynamic_update_slice_in_dim(user_total, old_users + user_part.reshape(panel_users, doubled), grid_row * panel_users, 0)
        old_items = lax.dynamic_slice_in_dim(item_total, grid_col, 1, 1)
        item_total = lax.dynamic_update_slice_in_dim(item_total, old_items + item_part.reshape(N_ROW, 1, ID, doubled), grid_col, 1)
        return (user_total, item_total)
    start_users = jnp.zeros((USERS, doubled), jnp.float32)
    start_items = jnp.zeros((N_ROW, N_COL, ID, doubled), jnp.float32)
    user_total, item_total = lax.fori_loop(0, N_ROW * N_COL, visit_device, (start_users, start_items))
    item_total = item_total.reshape(ITEMS, doubled)
    user_out = user_total * user_root[:, None]
    item_out = item_total * item_root[:, None]
    return (user_out[:, :FEAT], item_out[:, :FEAT], user_out[:, FEAT:], item_out[:, FEAT:])
```

```python
import jax
import jax.numpy as jnp
from jax import lax
from jax.experimental import pallas as pl
from jax.experimental.pallas import tpu as pltpu
from jax.sharding import PartitionSpec as P

BF16 = jnp.bfloat16
F32 = jnp.float32
MESH = pl.DeviceIdType.MESH
ANY = pl.BlockSpec(memory_space=pl.ANY)
VM = pl.BlockSpec(memory_space=pltpu.VMEM)

BLOCK = 128
SHARD = 256
HALF = 128
WIDTH = 256
RING = 4
USERS = 4096
ITEMS = 2048
SLOTS = 10
ROWS = 32
COLS = 16
STEPS = 8


def layer_kernel(
    user_emb, item_emb, user_cot, item_cot, tiles, tile_cols, row_count, user_deg, item_deg,
    user_next, item_next, user_grad, item_grad,
    slot_tiles, dense, user_panel, item_panel, raw, degs, cols_v, count_v, place_v, place_s, roots,
    user_acc, item_acc, core_send, core_recv,
    z_send, z_relay, z_recv, x_send, x_recv,
    y_send, y_relay, y_recv, h_send, h_recv,
    load_sem, tile_sem, place_sem, send_sem,
    up_sem, ip_sem, core_sem, zrelay_sem, z_sem, x_sem, yrelay_sem, y_sem, h_sem,
):
    row, col = lax.axis_index("row"), lax.axis_index("col")
    xh, y = row // RING, row % RING
    z, xl, core = col // RING, (col // 2) % 2, col % 2
    yr, ylf = (y + 1) % RING, (y + 3) % RING
    zr, zlf = (z + 1) % RING, (z + 3) % RING

    def dev(xh_=xh, y_=y, z_=z, xl_=xl, core_=core):
        return (xh_ * RING + y_, z_ * RING + xl_ * 2 + core_)

    d_core = dev(core_=1 - core)
    d_x = dev(xl_=1 - xl)
    d_zr, d_zl = dev(z_=zr), dev(z_=zlf)
    d_h = dev(xh_=1 - xh)
    d_yr, d_yl = dev(y_=yr), dev(y_=ylf)
    peers = (d_core, d_x, d_zr, d_zl, d_h, d_yr, d_yl)

    def copy(src, dst, ssem, rsem, device):
        return pltpu.make_async_remote_copy(
            src_ref=src, dst_ref=dst, send_sem=ssem, recv_sem=rsem,
            device_id=device, device_id_type=MESH)

    loads = [
        pltpu.make_async_copy(src, dst, load_sem.at[i])
        for i, (src, dst) in enumerate((
            (user_emb, raw.at[0]), (user_cot, raw.at[1]),
            (item_emb, raw.at[2]), (item_cot, raw.at[3]),
            (user_deg, degs.at[0]), (item_deg, degs.at[1]),
            (tile_cols, cols_v), (row_count, count_v)))
    ]
    for load in loads:
        load.start()
    barrier = pltpu.get_barrier_semaphore()
    for peer in peers:
        pl.semaphore_signal(barrier, inc=1, device_id=peer, device_id_type=MESH)
    fetches = [
        pltpu.make_async_copy(
            tiles.at[:, pl.ds(k * BLOCK, BLOCK)], slot_tiles.at[k], tile_sem.at[k])
        for k in range(SLOTS)
    ]
    for load in loads:
        load.wait()
    for fetch in fetches:
        fetch.start()

    diag = (lax.broadcasted_iota(jnp.int32, (BLOCK, BLOCK), 0)
            == lax.broadcasted_iota(jnp.int32, (BLOCK, BLOCK), 1))
    for kind in range(2):
        root = 1.0 / jnp.sqrt(degs[kind].astype(F32))
        for part in range(2):
            wide = jnp.broadcast_to(root[part:part + 1, :], (BLOCK, BLOCK))
            column = jnp.sum(jnp.where(diag, wide, 0.0), axis=1, keepdims=True)
            roots[kind, part * BLOCK:(part + 1) * BLOCK, :] = jnp.broadcast_to(column, (BLOCK, BLOCK))

    def scaled(kind, value):
        r = roots[kind]
        return value * jnp.concatenate([r, r], axis=1)

    own_user = col * SHARD
    own_item = row * SHARD
    for f in range(2):
        user_panel[f, pl.ds(own_user, SHARD), :] = scaled(0, raw[f].astype(F32)).astype(BF16)
        item_panel[f, pl.ds(own_item, SHARD), :] = scaled(1, raw[2 + f].astype(F32)).astype(BF16)

    blocks = lax.broadcasted_iota(jnp.int32, (ROWS, COLS), 1)
    live = jnp.broadcast_to(count_v[...], (ROWS, COLS))
    place = jnp.full((ROWS, COLS), SLOTS, jnp.int32)
    for k in range(SLOTS):
        named = jnp.broadcast_to(cols_v[:, k:k + 1], (ROWS, COLS))
        place = jnp.where((named == blocks) & (live > k), k, place)
    place_v[...] = place
    to_scalar = pltpu.make_async_copy(place_v, place_s, place_sem)
    to_scalar.start()

    pl.semaphore_wait(barrier, len(peers))

    def u_piece(f, z_, x_, c_, h):
        slot = z_ * RING + x_ * 2 + c_
        return user_panel.at[f, pl.ds(slot * SHARD + h * HALF, HALF)], up_sem.at[f, slot * 2 + h]

    def i_piece(f, xh_, y_, h):
        slot = xh_ * RING + y_
        return item_panel.at[f, pl.ds(slot * SHARD + h * HALF, HALF)], ip_sem.at[f, slot * 2 + h]

    def u_send(f, piece, device):
        ref, sem = piece
        copy(ref, ref, send_sem.at[0, f], sem, device).start()

    def i_send(f, piece, device):
        ref, sem = piece
        copy(ref, ref, send_sem.at[1, f], sem, device).start()

    def arrived(f, piece):
        ref, sem = piece
        copy(ref, ref, send_sem.at[0, f], sem, d_core).wait_recv()

    xp, hp = 1 - xl, 1 - xh

    def gather_own(f):
        for h in range(2):
            u_send(f, u_piece(f, z, xl, core, h), d_x)
            i_send(f, i_piece(f, xh, y, h), d_h)
        for h in range(2):
            u_send(f, u_piece(f, z, xl, core, h), d_zr)
            u_send(f, u_piece(f, z, xl, core, 1 - h), d_zl)
            i_send(f, i_piece(f, xh, y, h), d_yr)
            i_send(f, i_piece(f, xh, y, 1 - h), d_yl)
        for h in range(2):
            u_send(f, u_piece(f, z, xl, core, h), d_core)

    def gather_partner(f):
        for h in range(2):
            piece = u_piece(f, z, xp, core, h)
            arrived(f, piece)
            u_send(f, piece, d_zr)
            u_send(f, piece, d_zl)
            u_send(f, piece, d_core)
        for h in range(2):
            piece = i_piece(f, hp, y, h)
            arrived(f, piece)
            i_send(f, piece, d_yr)
            i_send(f, piece, d_yl)

    def gather_forward(f, x_, h_):
        left, right = u_piece(f, zlf, x_, core, 0), u_piece(f, zr, x_, core, 1)
        arrived(f, left)
        u_send(f, left, d_zr)
        u_send(f, left, d_core)
        arrived(f, right)
        u_send(f, right, d_zl)
        u_send(f, right, d_core)
        left, right = i_piece(f, h_, ylf, 0), i_piece(f, h_, yr, 1)
        arrived(f, left)
        i_send(f, left, d_yr)
        arrived(f, right)
        i_send(f, right, d_yl)

    def gather_rest(f):
        for x_, h_ in ((xl, xh), (xp, hp)):
            for piece in (u_piece(f, zlf, x_, core, 1), u_piece(f, zr, x_, core, 0)):
                arrived(f, piece)
                u_send(f, piece, d_core)
            arrived(f, i_piece(f, h_, ylf, 1))
            arrived(f, i_piece(f, h_, yr, 0))

    def gather_far(f):
        far_z, far_y = (z + 2) % RING, (y + 2) % RING
        for x_, h_ in ((xl, xh), (xp, hp)):
            for h in range(2):
                piece = u_piece(f, far_z, x_, core, h)
                arrived(f, piece)
                u_send(f, piece, d_core)
                arrived(f, i_piece(f, h_, far_y, h))

    def gather_end(f):
        for dz in (0, 1, 3, 2):
            for x_ in (xl, xp):
                for h in range(2):
                    arrived(f, u_piece(f, (z + dz) % RING, x_, 1 - core, h))

    gather_own(0)
    slot_tiles[SLOTS] = jnp.zeros((USERS, BLOCK), BF16)
    to_scalar.wait()
    for fetch in fetches:
        fetch.wait()

    def spread(start, stop):
        def body(b, carry):
            r = pl.multiple_of(b * BLOCK, BLOCK)
            for c in range(COLS):
                dense[pl.ds(r, BLOCK), c * BLOCK:(c + 1) * BLOCK] = slot_tiles[place_s[b, c], pl.ds(r, BLOCK), :]
            return carry
        lax.fori_loop(start, stop, body, 0)

    gather_partner(0)
    spread(0, 8)
    gather_forward(0, xl, xh)
    spread(8, 16)
    gather_forward(0, xp, hp)
    gather_own(1)
    spread(16, 32)
    gather_rest(0)
    gather_partner(1)
    gather_far(0)
    gather_end(0)

    def user_far(f, k, xs):
        z_send[f, k] = (user_acc[k, 0] + core_recv[f, k].astype(F32)).astype(BF16)
        for h, device in ((0, d_zr), (1, d_zl)):
            copy(z_send.at[f, k, pl.ds(h * HALF, HALF)], z_relay.at[f, xs, h],
                 send_sem.at[2, f], zrelay_sem.at[f, xs * 2 + h], device).start()

    def user_near(f, k, xs, h, device):
        total = user_acc[k, 0] + core_recv[f, k].astype(F32)
        relay = z_relay.at[f, xs, h]
        copy(relay, relay, send_sem.at[2, f], zrelay_sem.at[f, xs * 2 + h], device).wait_recv()
        passed = relay[...].astype(F32)
        top = total[:HALF] + passed if h == 0 else total[:HALF]
        low = total[HALF:] + passed if h == 1 else total[HALF:]
        z_send[f, k, 0:HALF, :] = top.astype(BF16)
        z_send[f, k, HALF:SHARD, :] = low.astype(BF16)
        copy(z_send.at[f, k], z_recv.at[f, xs, h], send_sem.at[2, f],
             z_sem.at[f, xs * 2 + h], device).start()

    def core_arrived(f, k):
        ref = core_recv.at[f, k]
        copy(ref, ref, send_sem.at[2, f], core_sem.at[f * STEPS + k], d_core).wait_recv()

    def item_far(f, k, xs):
        y_send[f, k] = item_acc[k].astype(BF16)
        for h, device in ((0, d_yr), (1, d_yl)):
            copy(y_send.at[f, k, pl.ds(h * HALF, HALF)], y_relay.at[f, xs, h],
                 send_sem.at[3, f], yrelay_sem.at[f, xs * 2 + h], device).start()

    def item_near(f, k, xs, h, device):
        relay = y_relay.at[f, xs, h]
        copy(relay, relay, send_sem.at[3, f], yrelay_sem.at[f, xs * 2 + h], device).wait_recv()
        passed = relay[...].astype(F32)
        total = item_acc[k]
        top = total[:HALF] + passed if h == 0 else total[:HALF]
        low = total[HALF:] + passed if h == 1 else total[HALF:]
        y_send[f, k, 0:HALF, :] = top.astype(BF16)
        y_send[f, k, HALF:SHARD, :] = low.astype(BF16)
        copy(y_send.at[f, k], y_recv.at[f, xs, h], send_sem.at[3, f],
             y_sem.at[f, xs * 2 + h], device).start()

    user_out, item_out = (user_next, user_grad), (item_next, item_grad)

    def cross(f):
        for h in range(2):
            ref = z_recv.at[f, 1, h]
            copy(ref, ref, send_sem.at[2, f], z_sem.at[f, 2 + h], d_core).wait_recv()
            ref = y_recv.at[f, 1, h]
            copy(ref, ref, send_sem.at[3, f], y_sem.at[f, 2 + h], d_core).wait_recv()
        x_send[f] = (user_acc[8 + f * 2 + 0, 0] + z_recv[f, 1, 0].astype(F32) + z_recv[f, 1, 1].astype(F32)).astype(BF16)
        copy(x_send.at[f], x_recv.at[f], send_sem.at[2, f], x_sem.at[f], d_x).start()
        h_send[f] = (item_acc[8 + f * 2 + 0] + y_recv[f, 1, 0].astype(F32) + y_recv[f, 1, 1].astype(F32)).astype(BF16)
        copy(h_send.at[f], h_recv.at[f], send_sem.at[3, f], h_sem.at[f], d_h).start()

    def finish(f):
        for h in range(2):
            ref = z_recv.at[f, 0, h]
            copy(ref, ref, send_sem.at[2, f], z_sem.at[f, h], d_core).wait_recv()
            ref = y_recv.at[f, 0, h]
            copy(ref, ref, send_sem.at[3, f], y_sem.at[f, h], d_core).wait_recv()
        copy(x_recv.at[f], x_recv.at[f], send_sem.at[2, f], x_sem.at[f], d_x).wait_recv()
        total = (user_acc[8 + f * 2 + 1, 0] + z_recv[f, 0, 0].astype(F32) + z_recv[f, 0, 1].astype(F32)
                 + x_recv[f].astype(F32))
        user_out[f][...] = scaled(0, total)
        copy(h_recv.at[f], h_recv.at[f], send_sem.at[3, f], h_sem.at[f], d_h).wait_recv()
        total = (item_acc[8 + f * 2 + 1] + y_recv[f, 0, 0].astype(F32) + y_recv[f, 0, 1].astype(F32)
                 + h_recv[f].astype(F32))
        item_out[f][...] = scaled(1, total)

    def lagged(f, k):
        core_arrived(f, k)

        @pl.when(k < 2)
        def _():
            user_far(f, k, 1 - k)

        for kk, xs, h in ((2, 1, 0), (3, 1, 1), (4, 0, 0), (5, 0, 1)):
            @pl.when(k == kk)
            def _(kk=kk, xs=xs, h=h):
                user_near(f, kk, xs, h, d_zr if h == 0 else d_zl)
                item_near(f, kk, xs, h, d_yr if h == 0 else d_yl)

        @pl.when(k >= 6)
        def _():
            keep = 8 + f * 2 + k - 6
            user_acc[keep, 0] = user_acc[k, 0] + core_recv[f, k].astype(F32)
            item_acc[keep] = item_acc[k]

    def step(t, carry):
        f, k = t // STEPS, t % STEPS
        dz = jnp.where(k < 2, 2, jnp.where(k < 6, 1 + 2 * (k % 2), 0))
        xs = jnp.where(k < 2, 1 - k, jnp.where(k < 6, 1 - (k - 2) // 2, 7 - k))
        x_ = (xl + xs) % 2
        h_ = (xh + xs) % 2
        pair = ((z + dz) % RING) * 2 + x_
        rows = pl.multiple_of(pair * (2 * SHARD), 2 * SHARD)
        part = jnp.dot(dense[pl.ds(rows, 2 * SHARD), :], item_panel[f], preferred_element_type=F32)
        user_acc[k, core] = part[:SHARD]
        user_acc[k, 1 - core] = part[SHARD:]
        core_send[f, k] = user_acc[k, 1].astype(BF16)
        copy(core_send.at[f, k], core_recv.at[f, k], send_sem.at[2, f],
             core_sem.at[f * STEPS + k], d_core).start()
        block = h_ * RING + (y + dz) % RING
        columns = pl.multiple_of(block * SHARD, SHARD)
        item_acc[k] = lax.dot_general(
            dense[:, pl.ds(columns, SHARD)], user_panel[f], (((0,), (0,)), ((), ())),
            preferred_element_type=F32)

        @pl.when(k < 2)
        def _():
            item_far(f, k, 1 - k)

        @pl.when(t > 0)
        def _():
            lagged((t - 1) // STEPS, (t - 1) % STEPS)

        @pl.when(t == 0)
        def _():
            gather_forward(1, xl, xh)

        @pl.when(t == 1)
        def _():
            gather_forward(1, xp, hp)

        @pl.when(t == 3)
        def _():
            gather_rest(1)

        @pl.when(t == 5)
        def _():
            gather_far(1)

        @pl.when(t == 7)
        def _():
            gather_end(1)

        @pl.when(t == 9)
        def _():
            cross(0)

        @pl.when(t == 12)
        def _():
            finish(0)

        return carry

    lax.fori_loop(0, 2 * STEPS, step, 0)
    lagged(1, STEPS - 1)
    cross(1)
    finish(1)

    for f in range(2):
        for group, units in ((0, 30), (1, 14), (2, 30), (3, 14)):
            ref = user_panel.at[f, pl.ds(0, units * HALF)]
            copy(ref, ref, send_sem.at[group, f], up_sem.at[f, 0], d_core).wait_send()


def shards(user_emb, item_emb, user_cot, item_cot, tiles, tile_cols, row_count, user_deg, item_deg):
    out = jax.ShapeDtypeStruct((SHARD, WIDTH), F32)
    dma = pltpu.SemaphoreType.DMA
    square = (SHARD, WIDTH)
    piece = (HALF, WIDTH)
    return pl.pallas_call(
        layer_kernel,
        name="layer",
        out_shape=(out,) * 4,
        in_specs=[ANY] * 9,
        out_specs=(VM,) * 4,
        scratch_shapes=[
            pltpu.VMEM((SLOTS + 1, USERS, BLOCK), BF16),
            pltpu.VMEM((USERS, ITEMS), BF16),
            pltpu.VMEM((2, USERS, WIDTH), BF16),
            pltpu.VMEM((2, ITEMS, WIDTH), BF16),
            pltpu.VMEM((4,) + square, BF16),
            pltpu.VMEM((2, 2, BLOCK), jnp.int32),
            pltpu.VMEM((ROWS, SLOTS), jnp.int32),
            pltpu.VMEM((ROWS, 1), jnp.int32),
            pltpu.VMEM((ROWS, COLS), jnp.int32),
            pltpu.SMEM((ROWS, COLS), jnp.int32),
            pltpu.VMEM((2, SHARD, BLOCK), F32),
            pltpu.VMEM((12, 2) + square, F32),
            pltpu.VMEM((12,) + square, F32),
            pltpu.VMEM((2, STEPS) + square, BF16),
            pltpu.VMEM((2, STEPS) + square, BF16),
            pltpu.VMEM((2, 6) + square, BF16),
            pltpu.VMEM((2, 2, 2) + piece, BF16),
            pltpu.VMEM((2, 2, 2) + square, BF16),
            pltpu.VMEM((2,) + square, BF16),
            pltpu.VMEM((2,) + square, BF16),
            pltpu.VMEM((2, 6) + square, BF16),
            pltpu.VMEM((2, 2, 2) + piece, BF16),
            pltpu.VMEM((2, 2, 2) + square, BF16),
            pltpu.VMEM((2,) + square, BF16),
            pltpu.VMEM((2,) + square, BF16),
            dma((8,)), dma((SLOTS,)), dma, dma((4, 2)),
            dma((2, 32)), dma((2, 16)), dma((16,)), dma((2, 4)), dma((2, 4)), dma((2,)),
            dma((2, 4)), dma((2, 4)), dma((2,)),
        ],
        compiler_params=pltpu.CompilerParams(
            collective_id=0, has_side_effects=True, vmem_limit_bytes=62 << 20),
    )(user_emb, item_emb, user_cot, item_cot, tiles, tile_cols, row_count,
      user_deg.reshape(2, BLOCK), item_deg.reshape(2, BLOCK))


def solution(mesh):
    nodes = P(("row", "col"), None)
    in_specs = (nodes, nodes, nodes, nodes, P("row", "col"), P("row", "col"), P("row", "col"),
                P(("row", "col")), P(("row", "col")))
    return jax.shard_map(shards, mesh=mesh, in_specs=in_specs, out_specs=(nodes,) * 4, check_vma=False)
```

```python
import jax
import jax.numpy as jnp
from jax import lax
from jax.experimental import pallas as pl
from jax.experimental.pallas import tpu as pltpu
from jax.sharding import PartitionSpec as P

BF16 = jnp.bfloat16
F32 = jnp.float32
MESH = pl.DeviceIdType.MESH
ANY = pl.BlockSpec(memory_space=pl.ANY)
VM = pl.BlockSpec(memory_space=pltpu.VMEM)

BLOCK = 128
SHARD = 256
HALF = 128
WIDTH = 256
RING = 4
USERS = 4096
ITEMS = 2048
SLOTS = 10
ROWS = 32
COLS = 16
STEPS = 16
ORDER = (
    (0, 2, 1), (0, 2, 0), (0, 0, 1), (0, 1, 1), (0, 3, 1), (1, 2, 1), (0, 1, 0), (1, 2, 0),
    (1, 1, 1), (1, 3, 1), (0, 3, 0), (1, 0, 1), (1, 1, 0), (1, 3, 0), (0, 0, 0), (1, 0, 0),
)


def layer_kernel(
    user_emb, item_emb, user_cot, item_cot, tiles, tile_cols, row_count, user_deg, item_deg,
    user_next, item_next, user_grad, item_grad,
    slot_tiles, dense, user_panel, item_panel, raw, degs, cols_v, count_v, place_v, place_s, roots,
    user_acc, item_acc, core_send, core_recv,
    z_send, z_relay, z_recv, x_send, x_recv,
    y_send, y_relay, y_recv, h_send, h_recv,
    load_sem, tile_sem, place_sem, send_sem,
    up_sem, ip_sem, core_sem, zrelay_sem, z_sem, x_sem, yrelay_sem, y_sem, h_sem,
):
    row, col = lax.axis_index("row"), lax.axis_index("col")
    xh, y = row // RING, row % RING
    z, xl, core = col // RING, (col // 2) % 2, col % 2
    yr, ylf = (y + 1) % RING, (y + 3) % RING
    zr, zlf = (z + 1) % RING, (z + 3) % RING

    def dev(xh_=xh, y_=y, z_=z, xl_=xl, core_=core):
        return (xh_ * RING + y_, z_ * RING + xl_ * 2 + core_)

    d_core = dev(core_=1 - core)
    d_x = dev(xl_=1 - xl)
    d_zr, d_zl = dev(z_=zr), dev(z_=zlf)
    d_h = dev(xh_=1 - xh)
    d_yr, d_yl = dev(y_=yr), dev(y_=ylf)
    peers = (d_core, d_x, d_zr, d_zl, d_h, d_yr, d_yl)

    def copy(src, dst, ssem, rsem, device):
        return pltpu.make_async_remote_copy(
            src_ref=src, dst_ref=dst, send_sem=ssem, recv_sem=rsem,
            device_id=device, device_id_type=MESH)

    loads = [
        pltpu.make_async_copy(src, dst, load_sem.at[i])
        for i, (src, dst) in enumerate((
            (user_emb, raw.at[0]), (user_cot, raw.at[1]),
            (item_emb, raw.at[2]), (item_cot, raw.at[3]),
            (user_deg, degs.at[0]), (item_deg, degs.at[1]),
            (tile_cols, cols_v), (row_count, count_v)))
    ]
    for load in loads:
        load.start()
    barrier = pltpu.get_barrier_semaphore()
    for peer in peers:
        pl.semaphore_signal(barrier, inc=1, device_id=peer, device_id_type=MESH)
    fetches = [
        pltpu.make_async_copy(
            tiles.at[:, pl.ds(k * BLOCK, BLOCK)], slot_tiles.at[k], tile_sem.at[k])
        for k in range(SLOTS)
    ]
    for load in loads:
        load.wait()
    for fetch in fetches:
        fetch.start()

    diag = (lax.broadcasted_iota(jnp.int32, (BLOCK, BLOCK), 0)
            == lax.broadcasted_iota(jnp.int32, (BLOCK, BLOCK), 1))
    for kind in range(2):
        root = 1.0 / jnp.sqrt(degs[kind].astype(F32))
        for part in range(2):
            wide = jnp.broadcast_to(root[part:part + 1, :], (BLOCK, BLOCK))
            column = jnp.sum(jnp.where(diag, wide, 0.0), axis=1, keepdims=True)
            roots[kind, part * BLOCK:(part + 1) * BLOCK, :] = jnp.broadcast_to(column, (BLOCK, BLOCK))

    def scaled(kind, value):
        r = roots[kind]
        return value * jnp.concatenate([r, r], axis=1)

    own_user = col * SHARD
    own_item = row * SHARD
    for f in range(2):
        user_panel[f, pl.ds(own_user, SHARD), :] = scaled(0, raw[f].astype(F32)).astype(BF16)
        item_panel[f, pl.ds(own_item, SHARD), :] = scaled(1, raw[2 + f].astype(F32)).astype(BF16)

    blocks = lax.broadcasted_iota(jnp.int32, (COLS, ROWS), 0)
    live = jnp.broadcast_to(count_v[...], (COLS, ROWS))
    place = jnp.full((COLS, ROWS), SLOTS, jnp.int32)
    for k in range(SLOTS):
        named = jnp.broadcast_to(cols_v[k:k + 1, :], (COLS, ROWS))
        place = jnp.where((named == blocks) & (live > k), k, place)
    place_v[...] = place
    to_scalar = pltpu.make_async_copy(place_v, place_s, place_sem)
    to_scalar.start()

    pl.semaphore_wait(barrier, len(peers))

    xp, hp = 1 - xl, 1 - xh
    pair_x, pair_h = (xl, xp), (xh, hp)

    def u_piece(f, dz, q, h, c_=core):
        slot = ((z + dz) % RING) * RING + pair_x[q] * 2 + c_
        return user_panel.at[f, pl.ds(slot * SHARD + h * HALF, HALF)], up_sem.at[f, slot * 2 + h]

    def i_piece(f, dy, q, h):
        slot = pair_h[q] * RING + (y + dy) % RING
        return item_panel.at[f, pl.ds(slot * SHARD + h * HALF, HALF)], ip_sem.at[f, slot * 2 + h]

    def send(group, f, piece, *devices):
        ref, sem = piece
        for device in devices:
            copy(ref, ref, send_sem.at[group, f], sem, device).start()

    def arrived(piece):
        ref, sem = piece
        copy(ref, ref, send_sem.at[0, 0], sem, d_core).wait_recv()

    def own_across(f, h):
        send(0, f, u_piece(f, 0, 0, h), d_x)
        send(1, f, i_piece(f, 0, 0, h), d_h)

    def own_along(f):
        for h in range(2):
            send(0, f, u_piece(f, 0, 0, h), d_zr)
            send(0, f, u_piece(f, 0, 0, 1 - h), d_zl)
            send(1, f, i_piece(f, 0, 0, h), d_yr)
            send(1, f, i_piece(f, 0, 0, 1 - h), d_yl)
        for h in range(2):
            send(0, f, u_piece(f, 0, 0, h), d_core)

    def user_partner(f, h):
        piece = u_piece(f, 0, 1, h)
        arrived(piece)
        send(0, f, piece, d_zr, d_zl, d_core)

    def item_partner(f, h):
        piece = i_piece(f, 0, 1, h)
        arrived(piece)
        send(1, f, piece, d_yr, d_yl)

    def user_forward(f, q, h):
        piece = u_piece(f, 3 if h == 0 else 1, q, h)
        arrived(piece)
        send(0, f, piece, d_zr if h == 0 else d_zl, d_core)

    def item_forward(f, q, h):
        piece = i_piece(f, 3 if h == 0 else 1, q, h)
        arrived(piece)
        send(1, f, piece, d_yr if h == 0 else d_yl)

    def user_rest(f, q, h):
        piece = u_piece(f, 1 if h == 0 else 3, q, h)
        arrived(piece)
        send(0, f, piece, d_core)

    def user_far_here(f, q, h):
        piece = u_piece(f, 2, q, h)
        arrived(piece)
        send(0, f, piece, d_core)

    def gather_end(f):
        for q in range(2):
            for h in range(2):
                arrived(i_piece(f, 1 if h == 0 else 3, q, h))
                arrived(i_piece(f, 2, q, h))
        for dz in (0, 1, 3, 2):
            for q in range(2):
                for h in range(2):
                    arrived(u_piece(f, dz, q, h, 1 - core))

    for f in range(2):
        for h in range(2):
            own_across(f, h)
        own_along(f)
    slot_tiles[SLOTS] = jnp.zeros((USERS, BLOCK), BF16)
    to_scalar.wait()

    def spread(start, stop):
        def body(b, carry):
            r = pl.multiple_of(b * BLOCK, BLOCK)
            for c in range(COLS):
                dense[pl.ds(r, BLOCK), c * BLOCK:(c + 1) * BLOCK] = slot_tiles[place_s[c, b], pl.ds(r, BLOCK), :]
            return carry
        lax.fori_loop(start, stop, body, 0)

    for h in range(2):
        user_forward(0, 0, h)
        item_forward(0, 0, h)
    user_partner(0, 0)
    item_partner(0, 0)
    user_partner(0, 1)
    for fetch in fetches:
        fetch.wait()
    for h in range(2):
        user_rest(0, 0, h)
        user_forward(1, 0, h)
        item_forward(1, 0, h)
    item_partner(0, 1)
    spread(0, 6)
    for h in range(2):
        user_far_here(0, 0, h)
        user_forward(0, 1, h)
        item_forward(0, 1, h)
        spread(6 + 4 * h, 10 + 4 * h)
    user_partner(1, 0)
    item_partner(1, 0)
    for h in range(2):
        user_rest(1, 0, h)
        user_rest(0, 1, h)
    spread(14, 18)
    user_partner(1, 1)
    item_partner(1, 1)
    spread(18, 25)
    for h in range(2):
        user_far_here(0, 1, h)
    for h in range(2):
        user_far_here(1, 0, h)
    spread(25, 32)
    gather_end(0)

    def decode(t):
        f, dz, xs = 0, 0, 0
        for i, (f_, dz_, xs_) in enumerate(ORDER):
            at = (t == i).astype(jnp.int32)
            f, dz, xs = f + at * f_, dz + at * dz_, xs + at * xs_
        return f, dz, xs

    def take(ref, group, sem):
        copy(ref, ref, send_sem.at[group, 0], sem, d_core).wait_recv()

    def far(acc, f, t, xs, out, relay, group, sems, right, left):
        out[t] = acc.astype(BF16)
        for h, device in ((0, right), (1, left)):
            copy(out.at[t, pl.ds(h * HALF, HALF)], relay.at[f, xs, h],
                 send_sem.at[group, f], sems.at[f, xs * 2 + h], device).start()

    def near(acc, f, t, xs, h, out, relay, relay_sems, there, group, sems, device):
        take(relay.at[f, xs, h], group, relay_sems.at[f, xs * 2 + h])
        passed = relay[f, xs, h].astype(F32)
        top = acc[:HALF] + passed if h == 0 else acc[:HALF]
        low = acc[HALF:] + passed if h == 1 else acc[HALF:]
        out[t, 0:HALF, :] = top.astype(BF16)
        out[t, HALF:SHARD, :] = low.astype(BF16)
        copy(out.at[t], there.at[f, xs, h], send_sem.at[group, f], sems.at[f, xs * 2 + h], device).start()

    def user_sum(t):
        return user_acc[t] + core_recv[t].astype(F32)

    def lagged(t):
        f, dz, xs = decode(t)
        take(core_recv.at[t], 2, core_sem.at[t])

        @pl.when(dz == 2)
        def _():
            far(user_sum(t), f, t, xs, z_send, z_relay, 2, zrelay_sem, d_zr, d_zl)

        for dz_, h in ((1, 0), (3, 1)):
            @pl.when(dz == dz_)
            def _(h=h):
                near(user_sum(t), f, t, xs, h, z_send, z_relay, zrelay_sem, z_recv, 2, z_sem,
                     d_zr if h == 0 else d_zl)
                near(item_acc[t], f, t, xs, h, y_send, y_relay, yrelay_sem, y_recv, 3, y_sem,
                     d_yr if h == 0 else d_yl)

    user_out, item_out = (user_next, user_grad), (item_next, item_grad)

    def cross(f):
        t = ORDER.index((f, 0, 1))
        for h in range(2):
            take(z_recv.at[f, 1, h], 2, z_sem.at[f, 2 + h])
        x_send[f] = (user_sum(t) + z_recv[f, 1, 0].astype(F32) + z_recv[f, 1, 1].astype(F32)).astype(BF16)
        copy(x_send.at[f], x_recv.at[f], send_sem.at[2, f], x_sem.at[f], d_x).start()
        for h in range(2):
            take(y_recv.at[f, 1, h], 3, y_sem.at[f, 2 + h])
        h_send[f] = (item_acc[t] + y_recv[f, 1, 0].astype(F32) + y_recv[f, 1, 1].astype(F32)).astype(BF16)
        copy(h_send.at[f], h_recv.at[f], send_sem.at[3, f], h_sem.at[f], d_h).start()

    def finish(f):
        t = ORDER.index((f, 0, 0))
        for h in range(2):
            take(z_recv.at[f, 0, h], 2, z_sem.at[f, h])
        take(x_recv.at[f], 2, x_sem.at[f])
        total = (user_sum(t) + z_recv[f, 0, 0].astype(F32) + z_recv[f, 0, 1].astype(F32)
                 + x_recv[f].astype(F32))
        user_out[f][...] = scaled(0, total)
        for h in range(2):
            take(y_recv.at[f, 0, h], 3, y_sem.at[f, h])
        take(h_recv.at[f], 3, h_sem.at[f])
        total = (item_acc[t] + y_recv[f, 0, 0].astype(F32) + y_recv[f, 0, 1].astype(F32)
                 + h_recv[f].astype(F32))
        item_out[f][...] = scaled(1, total)

    def step(t, carry):
        f, dz, xs = decode(t)
        pair = ((z + dz) % RING) * 2 + (xl + xs) % 2
        mine = pl.multiple_of((pair * 2 + core) * SHARD, SHARD)
        other = pl.multiple_of((pair * 2 + 1 - core) * SHARD, SHARD)
        rows = jnp.concatenate([dense[pl.ds(mine, SHARD), :], dense[pl.ds(other, SHARD), :]], axis=0)
        part = jnp.dot(rows, item_panel[f], preferred_element_type=F32)
        user_acc[t] = part[:SHARD]
        core_send[t] = part[SHARD:].astype(BF16)
        block = ((xh + xs) % 2) * RING + (y + dz) % RING
        columns = pl.multiple_of(block * SHARD, SHARD)
        item_acc[t] = lax.dot_general(
            dense[:, pl.ds(columns, SHARD)], user_panel[f], (((0,), (0,)), ((), ())),
            preferred_element_type=F32)
        copy(core_send.at[t], core_recv.at[t], send_sem.at[2, f], core_sem.at[t], d_core).start()

        @pl.when(dz == 2)
        def _():
            far(item_acc[t], f, t, xs, y_send, y_relay, 3, yrelay_sem, d_yr, d_yl)

        @pl.when(t > 0)
        def _():
            lagged(t - 1)

        @pl.when(t == 0)
        def _():
            for h in range(2):
                user_forward(1, 1, h)
                item_forward(1, 1, h)

        @pl.when(t == 1)
        def _():
            for h in range(2):
                user_rest(1, 1, h)

        @pl.when(t == 3)
        def _():
            for h in range(2):
                user_far_here(1, 1, h)

        @pl.when(t == 4)
        def _():
            gather_end(1)

        @pl.when(t == 9)
        def _():
            cross(0)

        @pl.when(t == 13)
        def _():
            cross(1)

        return carry

    lax.fori_loop(0, STEPS, step, 0)
    take(core_recv.at[STEPS - 1], 2, core_sem.at[STEPS - 1])
    finish(0)
    finish(1)

    for f in range(2):
        for group, units in ((0, 30), (1, 14), (2, 30), (3, 14)):
            ref = user_panel.at[f, pl.ds(0, units * HALF)]
            copy(ref, ref, send_sem.at[group, f], up_sem.at[f, 0], d_core).wait_send()


def store_kernel(*refs):
    copies = [pltpu.make_async_copy(refs[i], refs[4 + i], refs[8].at[i]) for i in range(4)]
    for c in copies:
        c.start()
    for c in copies:
        c.wait()


def shards(user_emb, item_emb, user_cot, item_cot, tiles, tile_cols, row_count, user_deg, item_deg):
    out = jax.ShapeDtypeStruct((SHARD, WIDTH), F32)
    dma = pltpu.SemaphoreType.DMA
    square = (SHARD, WIDTH)
    piece = (HALF, WIDTH)
    results = pl.pallas_call(
        layer_kernel,
        name="layer",
        out_shape=(pltpu.VMEM((SHARD, WIDTH), F32),) * 4,
        in_specs=[ANY] * 9,
        out_specs=(VM,) * 4,
        scratch_shapes=[
            pltpu.VMEM((SLOTS + 1, USERS, BLOCK), BF16),
            pltpu.VMEM((USERS, ITEMS), BF16),
            pltpu.VMEM((2, USERS, WIDTH), BF16),
            pltpu.VMEM((2, ITEMS, WIDTH), BF16),
            pltpu.VMEM((4,) + square, BF16),
            pltpu.VMEM((2, 2, BLOCK), jnp.int32),
            pltpu.VMEM((SLOTS, ROWS), jnp.int32),
            pltpu.VMEM((1, ROWS), jnp.int32),
            pltpu.VMEM((COLS, ROWS), jnp.int32),
            pltpu.SMEM((COLS, ROWS), jnp.int32),
            pltpu.VMEM((2, SHARD, BLOCK), F32),
            pltpu.VMEM((STEPS,) + square, F32),
            pltpu.VMEM((STEPS,) + square, F32),
            pltpu.VMEM((STEPS,) + square, BF16),
            pltpu.VMEM((STEPS,) + square, BF16),
            pltpu.VMEM((STEPS,) + square, BF16),
            pltpu.VMEM((2, 2, 2) + piece, BF16),
            pltpu.VMEM((2, 2, 2) + square, BF16),
            pltpu.VMEM((2,) + square, BF16),
            pltpu.VMEM((2,) + square, BF16),
            pltpu.VMEM((STEPS,) + square, BF16),
            pltpu.VMEM((2, 2, 2) + piece, BF16),
            pltpu.VMEM((2, 2, 2) + square, BF16),
            pltpu.VMEM((2,) + square, BF16),
            pltpu.VMEM((2,) + square, BF16),
            dma((8,)), dma((SLOTS,)), dma, dma((4, 2)),
            dma((2, 32)), dma((2, 16)), dma((16,)), dma((2, 4)), dma((2, 4)), dma((2,)),
            dma((2, 4)), dma((2, 4)), dma((2,)),
        ],
        compiler_params=pltpu.CompilerParams(
            collective_id=0, has_side_effects=True, vmem_limit_bytes=62 << 20),
    )(user_emb, item_emb, user_cot, item_cot, tiles, tile_cols.T, row_count.T,
      user_deg.reshape(2, BLOCK), item_deg.reshape(2, BLOCK))
    return pl.pallas_call(
        store_kernel,
        name="store",
        out_shape=(out,) * 4,
        in_specs=[ANY] * 4,
        compiler_params=pltpu.CompilerParams(vmem_limit_bytes=1 << 20),
        out_specs=(ANY,) * 4,
        scratch_shapes=[dma((4,))],
    )(*results)


def solution(mesh):
    nodes = P(("row", "col"), None)
    in_specs = (nodes, nodes, nodes, nodes, P("row", "col"), P("row", "col"), P("row", "col"),
                P(("row", "col")), P(("row", "col")))
    return jax.shard_map(shards, mesh=mesh, in_specs=in_specs, out_specs=(nodes,) * 4, check_vma=False)
```

```python
import jax
import jax.numpy as jnp
from jax import lax
from jax.experimental import pallas as pl
from jax.experimental.pallas import tpu as pltpu
from jax.sharding import PartitionSpec as P

BF16 = jnp.bfloat16
F32 = jnp.float32
MESH = pl.DeviceIdType.MESH
ANY = pl.BlockSpec(memory_space=pl.ANY)
VM = pl.BlockSpec(memory_space=pltpu.VMEM)

BLOCK = 128
SHARD = 256
HALF = 128
WIDTH = 256
RING = 4
USERS = 4096
ITEMS = 2048
SLOTS = 10
ROWS = 32
COLS = 16
STEPS = 16
ORDER = (
    (0, 2, 1), (0, 2, 0), (0, 0, 1), (0, 1, 1), (0, 3, 1), (1, 2, 1), (0, 1, 0), (1, 2, 0),
    (1, 1, 1), (1, 3, 1), (0, 3, 0), (1, 0, 1), (1, 1, 0), (1, 3, 0), (0, 0, 0), (1, 0, 0),
)
FIRST = {1: 0, 2: 1, 4: 3, 5: 4, 6: 5, 7: 6, 8: 7, 9: 8, 10: 9, 11: 10, 13: 12, 14: 13}
SECOND = {4: 3, 5: 4, 7: 6, 9: 8, 10: 9, 11: 10, 13: 12, 14: 13}


def layer_kernel(
    user_emb, item_emb, user_cot, item_cot, tiles, tile_cols, row_count, user_deg, item_deg,
    user_next, item_next, user_grad, item_grad,
    slot_tiles, dense, user_panel, item_panel, raw, degs, cols_v, count_v, place_v, place_s, roots,
    user_acc, item_acc, core_send, core_recv,
    z_send, z_relay, z_recv, x_send, x_recv,
    y_send, y_relay, y_recv, h_send, h_recv,
    load_sem, tile_sem, place_sem, send_sem,
    up_sem, ip_sem, core_sem, zrelay_sem, z_sem, x_sem, yrelay_sem, y_sem, h_sem,
):
    row, col = lax.axis_index("row"), lax.axis_index("col")
    xh, y = row // RING, row % RING
    z, xl, core = col // RING, (col // 2) % 2, col % 2
    yr, ylf = (y + 1) % RING, (y + 3) % RING
    zr, zlf = (z + 1) % RING, (z + 3) % RING

    def dev(xh_=xh, y_=y, z_=z, xl_=xl, core_=core):
        return (xh_ * RING + y_, z_ * RING + xl_ * 2 + core_)

    d_core = dev(core_=1 - core)
    d_x = dev(xl_=1 - xl)
    d_zr, d_zl = dev(z_=zr), dev(z_=zlf)
    d_h = dev(xh_=1 - xh)
    d_yr, d_yl = dev(y_=yr), dev(y_=ylf)
    peers = (d_core, d_x, d_zr, d_zl, d_h, d_yr, d_yl)

    def copy(src, dst, ssem, rsem, device):
        return pltpu.make_async_remote_copy(
            src_ref=src, dst_ref=dst, send_sem=ssem, recv_sem=rsem,
            device_id=device, device_id_type=MESH)

    loads = [
        pltpu.make_async_copy(src, dst, load_sem.at[i])
        for i, (src, dst) in enumerate((
            (user_emb, raw.at[0]), (user_cot, raw.at[1]),
            (item_emb, raw.at[2]), (item_cot, raw.at[3]),
            (user_deg, degs.at[0]), (item_deg, degs.at[1]),
            (tile_cols, cols_v), (row_count, count_v)))
    ]
    for load in loads:
        load.start()
    barrier = pltpu.get_barrier_semaphore()
    for peer in peers:
        pl.semaphore_signal(barrier, inc=1, device_id=peer, device_id_type=MESH)
    fetches = [
        pltpu.make_async_copy(
            tiles.at[:, pl.ds(k * BLOCK, BLOCK)], slot_tiles.at[k], tile_sem.at[k])
        for k in range(SLOTS)
    ]
    for load in loads:
        load.wait()
    for fetch in fetches:
        fetch.start()

    diag = (lax.broadcasted_iota(jnp.int32, (BLOCK, BLOCK), 0)
            == lax.broadcasted_iota(jnp.int32, (BLOCK, BLOCK), 1))
    for kind in range(2):
        root = 1.0 / jnp.sqrt(degs[kind].astype(F32))
        for part in range(2):
            wide = jnp.broadcast_to(root[part:part + 1, :], (BLOCK, BLOCK))
            column = jnp.sum(jnp.where(diag, wide, 0.0), axis=1, keepdims=True)
            roots[kind, part * BLOCK:(part + 1) * BLOCK, :] = jnp.broadcast_to(column, (BLOCK, BLOCK))

    def scaled(kind, value):
        r = roots[kind]
        return value * jnp.concatenate([r, r], axis=1)

    own_user = col * SHARD
    own_item = row * SHARD
    for f in range(2):
        user_panel[f, pl.ds(own_user, SHARD), :] = scaled(0, raw[f].astype(F32)).astype(BF16)
        item_panel[f, pl.ds(own_item, SHARD), :] = scaled(1, raw[2 + f].astype(F32)).astype(BF16)

    blocks = lax.broadcasted_iota(jnp.int32, (COLS, ROWS), 0)
    live = jnp.broadcast_to(count_v[...], (COLS, ROWS))
    place = jnp.full((COLS, ROWS), SLOTS, jnp.int32)
    for k in range(SLOTS):
        named = jnp.broadcast_to(cols_v[k:k + 1, :], (COLS, ROWS))
        place = jnp.where((named == blocks) & (live > k), k, place)
    place_v[...] = place
    to_scalar = pltpu.make_async_copy(place_v, place_s, place_sem)
    to_scalar.start()

    pl.semaphore_wait(barrier, len(peers))

    xp, hp = 1 - xl, 1 - xh
    pair_x, pair_h = (xl, xp), (xh, hp)

    def u_piece(f, dz, q, h, c_=core):
        slot = ((z + dz) % RING) * RING + pair_x[q] * 2 + c_
        return user_panel.at[f, pl.ds(slot * SHARD + h * HALF, HALF)], up_sem.at[f, slot * 2 + h]

    def i_piece(f, dy, q, h):
        slot = pair_h[q] * RING + (y + dy) % RING
        return item_panel.at[f, pl.ds(slot * SHARD + h * HALF, HALF)], ip_sem.at[f, slot * 2 + h]

    def send(group, f, piece, *devices):
        ref, sem = piece
        for device in devices:
            copy(ref, ref, send_sem.at[group, f], sem, device).start()

    def arrived(piece):
        ref, sem = piece
        copy(ref, ref, send_sem.at[0, 0], sem, d_core).wait_recv()

    def own_across(f, h):
        send(0, f, u_piece(f, 0, 0, h), d_x)
        send(1, f, i_piece(f, 0, 0, h), d_h)

    def own_along(f):
        for h in range(2):
            send(0, f, u_piece(f, 0, 0, h), d_zr)
            send(0, f, u_piece(f, 0, 0, 1 - h), d_zl)
            send(1, f, i_piece(f, 0, 0, h), d_yr)
            send(1, f, i_piece(f, 0, 0, 1 - h), d_yl)
        for h in range(2):
            send(0, f, u_piece(f, 0, 0, h), d_core)

    def user_partner(f, h):
        piece = u_piece(f, 0, 1, h)
        arrived(piece)
        send(0, f, piece, d_zr, d_zl, d_core)

    def item_partner(f, h):
        piece = i_piece(f, 0, 1, h)
        arrived(piece)
        send(1, f, piece, d_yr, d_yl)

    def user_forward(f, q, h):
        piece = u_piece(f, 3 if h == 0 else 1, q, h)
        arrived(piece)
        send(0, f, piece, d_zr if h == 0 else d_zl, d_core)

    def item_forward(f, q, h):
        piece = i_piece(f, 3 if h == 0 else 1, q, h)
        arrived(piece)
        send(1, f, piece, d_yr if h == 0 else d_yl)

    def user_rest(f, q, h):
        piece = u_piece(f, 1 if h == 0 else 3, q, h)
        arrived(piece)
        send(0, f, piece, d_core)

    def user_far_here(f, q, h):
        piece = u_piece(f, 2, q, h)
        arrived(piece)
        send(0, f, piece, d_core)

    def gather_end(f):
        for q in range(2):
            for h in range(2):
                arrived(i_piece(f, 1 if h == 0 else 3, q, h))
                arrived(i_piece(f, 2, q, h))
        for dz in (0, 1, 3, 2):
            for q in range(2):
                for h in range(2):
                    arrived(u_piece(f, dz, q, h, 1 - core))

    for f in range(2):
        for h in range(2):
            own_across(f, h)
        own_along(f)
    slot_tiles[SLOTS] = jnp.zeros((USERS, BLOCK), BF16)
    to_scalar.wait()

    def spread(start, stop):
        def body(b, carry):
            r = pl.multiple_of(b * BLOCK, BLOCK)
            for c in range(COLS):
                dense[pl.ds(r, BLOCK), c * BLOCK:(c + 1) * BLOCK] = slot_tiles[place_s[c, b], pl.ds(r, BLOCK), :]
            return carry
        lax.fori_loop(start, stop, body, 0)

    for h in range(2):
        user_forward(0, 0, h)
        item_forward(0, 0, h)
    user_partner(0, 0)
    item_partner(0, 0)
    user_partner(0, 1)
    for fetch in fetches:
        fetch.wait()
    for h in range(2):
        user_rest(0, 0, h)
        user_forward(1, 0, h)
        item_forward(1, 0, h)
    item_partner(0, 1)
    spread(0, 6)
    for h in range(2):
        user_far_here(0, 0, h)
        user_forward(0, 1, h)
        item_forward(0, 1, h)
        spread(6 + 4 * h, 10 + 4 * h)
    user_partner(1, 0)
    item_partner(1, 0)
    for h in range(2):
        user_rest(1, 0, h)
        user_rest(0, 1, h)
    spread(14, 18)
    user_partner(1, 1)
    item_partner(1, 1)
    spread(18, 25)
    for h in range(2):
        user_far_here(0, 1, h)
    for h in range(2):
        user_far_here(1, 0, h)
    spread(25, 32)
    gather_end(0)

    def take(ref, group, sem):
        copy(ref, ref, send_sem.at[group, 0], sem, d_core).wait_recv()

    def half(h):
        return pl.ds(h * HALF, HALF)

    user_way = (user_acc, z_send, z_relay, z_recv, 2, zrelay_sem, z_sem, (d_zr, d_zl))
    item_way = (item_acc, y_send, y_relay, y_recv, 3, yrelay_sem, y_sem, (d_yr, d_yl))

    def send_first(way, t):
        f, dz, xs = ORDER[t]
        acc, out, relay, there, group, relay_sems, sems, devices = way
        if dz == 2:
            out[t] = acc[t].astype(BF16)
            for h in range(2):
                copy(out.at[t, half(h)], relay.at[f, xs, h], send_sem.at[group, f],
                     relay_sems.at[f, xs * 2 + h], devices[h]).start()
        elif dz:
            h = dz // 2
            other = 1 - h
            out[t, half(other), :] = acc[t, half(other), :].astype(BF16)
            copy(out.at[t, half(other)], there.at[f, xs, h, half(other)], send_sem.at[group, f],
                 sems.at[f, xs * 4 + h * 2 + other], devices[h]).start()

    def send_second(way, t):
        f, dz, xs = ORDER[t]
        acc, out, relay, there, group, relay_sems, sems, devices = way
        h = dz // 2
        take(relay.at[f, xs, h], group, relay_sems.at[f, xs * 2 + h])
        out[t, half(h), :] = (acc[t, half(h), :] + relay[f, xs, h].astype(F32)).astype(BF16)
        copy(out.at[t, half(h)], there.at[f, xs, h, half(h)], send_sem.at[group, f],
             sems.at[f, xs * 4 + h * 2 + h], devices[h]).start()

    def ring_sum(way, t, f, xs, r):
        acc, out, relay, there, group, relay_sems, sems, devices = way
        for h in range(2):
            take(there.at[f, xs, h, half(r)], group, sems.at[f, xs * 4 + h * 2 + r])
        total = acc[t, half(r), :] + there[f, xs, 0, half(r), :].astype(F32)
        return total + there[f, xs, 1, half(r), :].astype(F32)

    def user_arrived(t):
        take(core_recv.at[t], 2, core_sem.at[t])
        user_acc[t] = user_acc[t] + core_recv[t].astype(F32)

    user_out, item_out = (user_next, user_grad), (item_next, item_grad)

    def cross(f):
        t = ORDER.index((f, 0, 1))
        user_arrived(t)
        for r in range(2):
            x_send[f, half(r), :] = ring_sum(user_way, t, f, 1, r).astype(BF16)
            copy(x_send.at[f, half(r)], x_recv.at[f, half(r)], send_sem.at[2, f], x_sem.at[f, r], d_x).start()
            h_send[f, half(r), :] = ring_sum(item_way, t, f, 1, r).astype(BF16)
            copy(h_send.at[f, half(r)], h_recv.at[f, half(r)], send_sem.at[3, f], h_sem.at[f, r], d_h).start()

    def finish(f):
        t = ORDER.index((f, 0, 0))
        user_arrived(t)
        for r in range(2):
            for kind, way, came, sem, outs in (
                    (0, user_way, x_recv, x_sem, user_out), (1, item_way, h_recv, h_sem, item_out)):
                total = ring_sum(way, t, f, 0, r)
                take(came.at[f, half(r)], 2 + kind, sem.at[f, r])
                total = total + came[f, half(r), :].astype(F32)
                root = roots[kind, half(r), :]
                outs[f][half(r), :] = total * jnp.concatenate([root, root], axis=1)

    def step(t):
        f, dz, xs = ORDER[t]
        pair = ((z + dz) % RING) * 2 + (xl + xs) % 2
        mine = pl.multiple_of((pair * 2 + core) * SHARD, SHARD)
        other = pl.multiple_of((pair * 2 + 1 - core) * SHARD, SHARD)
        rows = jnp.concatenate([dense[pl.ds(mine, SHARD), :], dense[pl.ds(other, SHARD), :]], axis=0)
        part = jnp.dot(rows, item_panel[f], preferred_element_type=F32)
        user_acc[t] = part[:SHARD]
        core_send[t] = part[SHARD:].astype(BF16)
        block = ((xh + xs) % 2) * RING + (y + dz) % RING
        columns = pl.multiple_of(block * SHARD, SHARD)
        item_acc[t] = lax.dot_general(
            dense[:, pl.ds(columns, SHARD)], user_panel[f], (((0,), (0,)), ((), ())),
            preferred_element_type=F32)
        copy(core_send.at[t], core_recv.at[t], send_sem.at[2, f], core_sem.at[t], d_core).start()
        send_first(item_way, t)
        if t in FIRST:
            user_arrived(FIRST[t])
            send_first(user_way, FIRST[t])
        if t in SECOND:
            send_second(user_way, SECOND[t])
            send_second(item_way, SECOND[t])

        if t == 0:
            for h in range(2):
                user_forward(1, 1, h)
                item_forward(1, 1, h)

        if t == 1:
            for h in range(2):
                user_rest(1, 1, h)

        if t == 3:
            for h in range(2):
                user_far_here(1, 1, h)

        if t == 4:
            gather_end(1)

        if t == 9:
            cross(0)

        if t == 13:
            cross(1)

    for t in range(STEPS):
        step(t)
    finish(0)
    finish(1)

    for f in range(2):
        for group, units in ((0, 30), (1, 14), (2, 30), (3, 14)):
            ref = user_panel.at[f, pl.ds(0, units * HALF)]
            copy(ref, ref, send_sem.at[group, f], up_sem.at[f, 0], d_core).wait_send()


def store_kernel(*refs):
    copies = [pltpu.make_async_copy(refs[i], refs[4 + i], refs[8].at[i]) for i in range(4)]
    for c in copies:
        c.start()
    for c in copies:
        c.wait()


def shards(user_emb, item_emb, user_cot, item_cot, tiles, tile_cols, row_count, user_deg, item_deg):
    out = jax.ShapeDtypeStruct((SHARD, WIDTH), F32)
    dma = pltpu.SemaphoreType.DMA
    square = (SHARD, WIDTH)
    piece = (HALF, WIDTH)
    results = pl.pallas_call(
        layer_kernel,
        name="layer",
        out_shape=(pltpu.VMEM((SHARD, WIDTH), F32),) * 4,
        in_specs=[ANY] * 9,
        out_specs=(VM,) * 4,
        scratch_shapes=[
            pltpu.VMEM((SLOTS + 1, USERS, BLOCK), BF16),
            pltpu.VMEM((USERS, ITEMS), BF16),
            pltpu.VMEM((2, USERS, WIDTH), BF16),
            pltpu.VMEM((2, ITEMS, WIDTH), BF16),
            pltpu.VMEM((4,) + square, BF16),
            pltpu.VMEM((2, 2, BLOCK), jnp.int32),
            pltpu.VMEM((SLOTS, ROWS), jnp.int32),
            pltpu.VMEM((1, ROWS), jnp.int32),
            pltpu.VMEM((COLS, ROWS), jnp.int32),
            pltpu.SMEM((COLS, ROWS), jnp.int32),
            pltpu.VMEM((2, SHARD, BLOCK), F32),
            pltpu.VMEM((STEPS,) + square, F32),
            pltpu.VMEM((STEPS,) + square, F32),
            pltpu.VMEM((STEPS,) + square, BF16),
            pltpu.VMEM((STEPS,) + square, BF16),
            pltpu.VMEM((STEPS,) + square, BF16),
            pltpu.VMEM((2, 2, 2) + piece, BF16),
            pltpu.VMEM((2, 2, 2) + square, BF16),
            pltpu.VMEM((2,) + square, BF16),
            pltpu.VMEM((2,) + square, BF16),
            pltpu.VMEM((STEPS,) + square, BF16),
            pltpu.VMEM((2, 2, 2) + piece, BF16),
            pltpu.VMEM((2, 2, 2) + square, BF16),
            pltpu.VMEM((2,) + square, BF16),
            pltpu.VMEM((2,) + square, BF16),
            dma((8,)), dma((SLOTS,)), dma, dma((4, 2)),
            dma((2, 32)), dma((2, 16)), dma((16,)), dma((2, 4)), dma((2, 8)), dma((2, 2)),
            dma((2, 4)), dma((2, 8)), dma((2, 2)),
        ],
        compiler_params=pltpu.CompilerParams(
            collective_id=0, has_side_effects=True, vmem_limit_bytes=62 << 20),
    )(user_emb, item_emb, user_cot, item_cot, tiles, tile_cols.T, row_count.T,
      user_deg.reshape(2, BLOCK), item_deg.reshape(2, BLOCK))
    return pl.pallas_call(
        store_kernel,
        name="store",
        out_shape=(out,) * 4,
        in_specs=[ANY] * 4,
        compiler_params=pltpu.CompilerParams(vmem_limit_bytes=1 << 20),
        out_specs=(ANY,) * 4,
        scratch_shapes=[dma((4,))],
    )(*results)


def solution(mesh):
    nodes = P(("row", "col"), None)
    in_specs = (nodes, nodes, nodes, nodes, P("row", "col"), P("row", "col"), P("row", "col"),
                P(("row", "col")), P(("row", "col")))
    return jax.shard_map(shards, mesh=mesh, in_specs=in_specs, out_specs=(nodes,) * 4, check_vma=False)
```

```python
import jax
import jax.numpy as jnp
from jax import lax
from jax.experimental import pallas as pl
from jax.experimental.pallas import tpu as pltpu
from jax.sharding import PartitionSpec as P

BF16 = jnp.bfloat16
F32 = jnp.float32
MESH = pl.DeviceIdType.MESH
ANY = pl.BlockSpec(memory_space=pl.ANY)
VM = pl.BlockSpec(memory_space=pltpu.VMEM)

BLOCK = 128
SHARD = 256
HALF = 128
WIDTH = 256
RING = 4
USERS = 4096
ITEMS = 2048
SLOTS = 10
ROWS = 32
COLS = 16
STEPS = 16
ORDER = (
    (0, 2, 1), (0, 2, 0), (0, 0, 1), (0, 1, 1), (0, 3, 1), (1, 2, 1), (0, 1, 0), (1, 2, 0),
    (1, 1, 1), (1, 3, 1), (0, 3, 0), (1, 0, 1), (1, 1, 0), (1, 3, 0), (0, 0, 0), (1, 0, 0),
)
FIRST = {1: 0, 2: 1, 4: 3, 5: 4, 6: 5, 7: 6, 8: 7, 9: 8, 10: 9, 11: 10, 13: 12, 14: 13}
SECOND = {4: 3, 5: 4, 7: 6, 9: 8, 10: 9, 11: 10, 13: 12, 14: 13}


def layer_kernel(
    user_emb, item_emb, user_cot, item_cot, tiles, tile_cols, row_count, user_deg, item_deg,
    user_next, item_next, user_grad, item_grad,
    slot_tiles, dense, user_panel, item_panel, raw, degs, cols_v, count_v, place_v, place_s, roots,
    user_acc, item_acc, core_send, core_recv,
    z_send, z_relay, z_recv, x_send, x_recv,
    y_send, y_relay, y_recv, h_send, h_recv,
    load_sem, tile_sem, place_sem, send_sem,
    up_sem, ip_sem, core_sem, zrelay_sem, z_sem, x_sem, yrelay_sem, y_sem, h_sem,
):
    row, col = lax.axis_index("row"), lax.axis_index("col")
    xh, y = row // RING, row % RING
    z, xl, core = col // RING, (col // 2) % 2, col % 2
    yr, ylf = (y + 1) % RING, (y + 3) % RING
    zr, zlf = (z + 1) % RING, (z + 3) % RING

    def dev(xh_=xh, y_=y, z_=z, xl_=xl, core_=core):
        return (xh_ * RING + y_, z_ * RING + xl_ * 2 + core_)

    d_core = dev(core_=1 - core)
    d_x = dev(xl_=1 - xl)
    d_zr, d_zl = dev(z_=zr), dev(z_=zlf)
    d_h = dev(xh_=1 - xh)
    d_yr, d_yl = dev(y_=yr), dev(y_=ylf)
    peers = (d_core, d_x, d_zr, d_zl, d_h, d_yr, d_yl)

    def copy(src, dst, ssem, rsem, device):
        return pltpu.make_async_remote_copy(
            src_ref=src, dst_ref=dst, send_sem=ssem, recv_sem=rsem,
            device_id=device, device_id_type=MESH)

    loads = [
        pltpu.make_async_copy(src, dst, load_sem.at[i])
        for i, (src, dst) in enumerate((
            (user_emb, raw.at[0]), (user_cot, raw.at[1]),
            (item_emb, raw.at[2]), (item_cot, raw.at[3]),
            (user_deg, degs.at[0]), (item_deg, degs.at[1]),
            (tile_cols, cols_v), (row_count, count_v)))
    ]
    for load in loads:
        load.start()
    barrier = pltpu.get_barrier_semaphore()
    for peer in peers:
        pl.semaphore_signal(barrier, inc=1, device_id=peer, device_id_type=MESH)
    fetches = [
        pltpu.make_async_copy(
            tiles.at[:, pl.ds(k * BLOCK, BLOCK)], slot_tiles.at[k], tile_sem.at[k])
        for k in range(SLOTS)
    ]
    for load in loads:
        load.wait()
    for fetch in fetches:
        fetch.start()

    diag = (lax.broadcasted_iota(jnp.int32, (BLOCK, BLOCK), 0)
            == lax.broadcasted_iota(jnp.int32, (BLOCK, BLOCK), 1))
    for kind in range(2):
        root = 1.0 / jnp.sqrt(degs[kind].astype(F32))
        for part in range(2):
            wide = jnp.broadcast_to(root[part:part + 1, :], (BLOCK, BLOCK))
            column = jnp.sum(jnp.where(diag, wide, 0.0), axis=1, keepdims=True)
            roots[kind, part * BLOCK:(part + 1) * BLOCK, :] = jnp.broadcast_to(column, (BLOCK, BLOCK))

    def scaled(kind, value):
        r = roots[kind]
        return value * jnp.concatenate([r, r], axis=1)

    own_user = col * SHARD
    own_item = row * SHARD
    for f in range(2):
        user_panel[f, pl.ds(own_user, SHARD), :] = scaled(0, raw[f].astype(F32)).astype(BF16)
        item_panel[f, pl.ds(own_item, SHARD), :] = scaled(1, raw[2 + f].astype(F32)).astype(BF16)

    blocks = lax.broadcasted_iota(jnp.int32, (COLS, ROWS), 0)
    live = jnp.broadcast_to(count_v[...], (COLS, ROWS))
    place = jnp.full((COLS, ROWS), SLOTS, jnp.int32)
    for k in range(SLOTS):
        named = jnp.broadcast_to(cols_v[k:k + 1, :], (COLS, ROWS))
        place = jnp.where((named == blocks) & (live > k), k, place)
    place_v[...] = place
    to_scalar = pltpu.make_async_copy(place_v, place_s, place_sem)
    to_scalar.start()

    pl.semaphore_wait(barrier, len(peers))

    xp, hp = 1 - xl, 1 - xh
    pair_x, pair_h = (xl, xp), (xh, hp)

    def u_piece(f, dz, q, h, c_=core):
        slot = ((z + dz) % RING) * RING + pair_x[q] * 2 + c_
        return user_panel.at[f, pl.ds(slot * SHARD + h * HALF, HALF)], up_sem.at[f, slot * 2 + h]

    def i_piece(f, dy, q, h):
        slot = pair_h[q] * RING + (y + dy) % RING
        return item_panel.at[f, pl.ds(slot * SHARD + h * HALF, HALF)], ip_sem.at[f, slot * 2 + h]

    def send(group, f, piece, *devices):
        ref, sem = piece
        for device in devices:
            copy(ref, ref, send_sem.at[group, f], sem, device).start()

    def arrived(piece):
        ref, sem = piece
        copy(ref, ref, send_sem.at[0, 0], sem, d_core).wait_recv()

    def own_across(f, h):
        send(0, f, u_piece(f, 0, 0, h), d_x)
        send(1, f, i_piece(f, 0, 0, h), d_h)

    def own_along(f):
        for h in range(2):
            send(0, f, u_piece(f, 0, 0, h), d_zr)
            send(0, f, u_piece(f, 0, 0, 1 - h), d_zl)
            send(1, f, i_piece(f, 0, 0, h), d_yr)
            send(1, f, i_piece(f, 0, 0, 1 - h), d_yl)
        for h in range(2):
            send(0, f, u_piece(f, 0, 0, h), d_core)

    def user_partner(f, h):
        piece = u_piece(f, 0, 1, h)
        arrived(piece)
        send(0, f, piece, d_zr, d_zl, d_core)

    def item_partner(f, h):
        piece = i_piece(f, 0, 1, h)
        arrived(piece)
        send(1, f, piece, d_yr, d_yl)

    def user_forward(f, q, h):
        piece = u_piece(f, 3 if h == 0 else 1, q, h)
        arrived(piece)
        send(0, f, piece, d_zr if h == 0 else d_zl, d_core)

    def item_forward(f, q, h):
        piece = i_piece(f, 3 if h == 0 else 1, q, h)
        arrived(piece)
        send(1, f, piece, d_yr if h == 0 else d_yl)

    def user_rest(f, q, h):
        piece = u_piece(f, 1 if h == 0 else 3, q, h)
        arrived(piece)
        send(0, f, piece, d_core)

    def user_far_here(f, q, h):
        piece = u_piece(f, 2, q, h)
        arrived(piece)
        send(0, f, piece, d_core)

    def gather_end(f):
        for q in range(2):
            for h in range(2):
                arrived(i_piece(f, 1 if h == 0 else 3, q, h))
                arrived(i_piece(f, 2, q, h))
        for dz in (0, 1, 3, 2):
            for q in range(2):
                for h in range(2):
                    arrived(u_piece(f, dz, q, h, 1 - core))

    for f in range(2):
        for h in range(2):
            own_across(f, h)
        own_along(f)
    slot_tiles[SLOTS] = jnp.zeros((USERS, BLOCK), BF16)
    to_scalar.wait()

    def spread(start, stop):
        def body(b, carry):
            r = pl.multiple_of(b * BLOCK, BLOCK)
            for c in range(COLS):
                dense[pl.ds(r, BLOCK), c * BLOCK:(c + 1) * BLOCK] = slot_tiles[place_s[c, b], pl.ds(r, BLOCK), :]
            return carry
        lax.fori_loop(start, stop, body, 0)

    for h in range(2):
        user_forward(0, 0, h)
        item_forward(0, 0, h)
    user_partner(0, 0)
    item_partner(0, 0)
    user_partner(0, 1)
    for fetch in fetches:
        fetch.wait()
    for h in range(2):
        user_rest(0, 0, h)
        user_forward(1, 0, h)
        item_forward(1, 0, h)
    item_partner(0, 1)
    spread(0, 6)
    for h in range(2):
        user_far_here(0, 0, h)
        user_forward(0, 1, h)
        item_forward(0, 1, h)
        spread(6 + 4 * h, 10 + 4 * h)
    user_partner(1, 0)
    item_partner(1, 0)
    for h in range(2):
        user_rest(1, 0, h)
        user_rest(0, 1, h)
    spread(14, 18)
    user_partner(1, 1)
    item_partner(1, 1)
    spread(18, 25)
    for h in range(2):
        user_far_here(0, 1, h)
    for h in range(2):
        user_far_here(1, 0, h)
    spread(25, 32)
    gather_end(0)

    def take(ref, group, sem):
        copy(ref, ref, send_sem.at[group, 0], sem, d_core).wait_recv()

    def half(h):
        return pl.ds(h * HALF, HALF)

    user_way = (user_acc, z_send, z_relay, z_recv, 2, zrelay_sem, z_sem, (d_zr, d_zl))
    item_way = (item_acc, y_send, y_relay, y_recv, 3, yrelay_sem, y_sem, (d_yr, d_yl))

    def send_first(way, t):
        f, dz, xs = ORDER[t]
        acc, out, relay, there, group, relay_sems, sems, devices = way
        if dz == 2:
            out[t] = acc[t].astype(BF16)
            for h in range(2):
                copy(out.at[t, half(h)], relay.at[f, xs, h], send_sem.at[group, f],
                     relay_sems.at[f, xs * 2 + h], devices[h]).start()
        elif dz:
            h = dz // 2
            other = 1 - h
            out[t, half(other), :] = acc[t, half(other), :].astype(BF16)
            copy(out.at[t, half(other)], there.at[f, xs, h, half(other)], send_sem.at[group, f],
                 sems.at[f, xs * 4 + h * 2 + other], devices[h]).start()

    def send_second(way, t):
        f, dz, xs = ORDER[t]
        acc, out, relay, there, group, relay_sems, sems, devices = way
        h = dz // 2
        take(relay.at[f, xs, h], group, relay_sems.at[f, xs * 2 + h])
        out[t, half(h), :] = (acc[t, half(h), :] + relay[f, xs, h].astype(F32)).astype(BF16)
        copy(out.at[t, half(h)], there.at[f, xs, h, half(h)], send_sem.at[group, f],
             sems.at[f, xs * 4 + h * 2 + h], devices[h]).start()

    def ring_sum(way, t, f, xs, r):
        acc, out, relay, there, group, relay_sems, sems, devices = way
        for h in range(2):
            take(there.at[f, xs, h, half(r)], group, sems.at[f, xs * 4 + h * 2 + r])
        total = acc[t, half(r), :] + there[f, xs, 0, half(r), :].astype(F32)
        return total + there[f, xs, 1, half(r), :].astype(F32)

    def user_arrived(t):
        take(core_recv.at[t], 2, core_sem.at[t])
        user_acc[t] = user_acc[t] + core_recv[t].astype(F32)

    user_out, item_out = (user_next, user_grad), (item_next, item_grad)

    def cross(f):
        t = ORDER.index((f, 0, 1))
        user_arrived(t)
        for r in range(2):
            x_send[f, half(r), :] = ring_sum(user_way, t, f, 1, r).astype(BF16)
            copy(x_send.at[f, half(r)], x_recv.at[f, half(r)], send_sem.at[2, f], x_sem.at[f, r], d_x).start()
            h_send[f, half(r), :] = ring_sum(item_way, t, f, 1, r).astype(BF16)
            copy(h_send.at[f, half(r)], h_recv.at[f, half(r)], send_sem.at[3, f], h_sem.at[f, r], d_h).start()

    def finish(f):
        t = ORDER.index((f, 0, 0))
        user_arrived(t)
        for r in range(2):
            for kind, way, came, sem, outs in (
                    (0, user_way, x_recv, x_sem, user_out), (1, item_way, h_recv, h_sem, item_out)):
                total = ring_sum(way, t, f, 0, r)
                take(came.at[f, half(r)], 2 + kind, sem.at[f, r])
                total = total + came[f, half(r), :].astype(F32)
                root = roots[kind, half(r), :]
                outs[f][half(r), :] = total * jnp.concatenate([root, root], axis=1)

    def step(t):
        f, dz, xs = ORDER[t]
        pair = ((z + dz) % RING) * 2 + (xl + xs) % 2
        mine = pl.multiple_of((pair * 2 + core) * SHARD, SHARD)
        other = pl.multiple_of((pair * 2 + 1 - core) * SHARD, SHARD)
        rows = jnp.concatenate([dense[pl.ds(mine, SHARD), :], dense[pl.ds(other, SHARD), :]], axis=0)
        part = jnp.dot(rows, item_panel[f], preferred_element_type=F32)
        user_acc[t] = part[:SHARD]
        core_send[t] = part[SHARD:].astype(BF16)
        block = ((xh + xs) % 2) * RING + (y + dz) % RING
        columns = pl.multiple_of(block * SHARD, SHARD)
        item_acc[t] = lax.dot_general(
            dense[:, pl.ds(columns, SHARD)], user_panel[f], (((0,), (0,)), ((), ())),
            preferred_element_type=F32)
        copy(core_send.at[t], core_recv.at[t], send_sem.at[2, f], core_sem.at[t], d_core).start()
        send_first(item_way, t)
        if t in FIRST:
            user_arrived(FIRST[t])
            send_first(user_way, FIRST[t])
        if t in SECOND:
            send_second(user_way, SECOND[t])
            send_second(item_way, SECOND[t])

        if t == 0:
            for h in range(2):
                user_forward(1, 1, h)
                item_forward(1, 1, h)

        if t == 1:
            for h in range(2):
                user_rest(1, 1, h)

        if t == 3:
            for h in range(2):
                user_far_here(1, 1, h)

        if t == 4:
            gather_end(1)

        if t == 8:
            cross(0)

        if t == 12:
            cross(1)

    for t in range(STEPS):
        step(t)
    finish(0)
    finish(1)

    for f in range(2):
        for group, units in ((0, 30), (1, 14), (2, 30), (3, 14)):
            ref = user_panel.at[f, pl.ds(0, units * HALF)]
            copy(ref, ref, send_sem.at[group, f], up_sem.at[f, 0], d_core).wait_send()


def store_kernel(*refs):
    copies = [pltpu.make_async_copy(refs[i], refs[4 + i], refs[8].at[i]) for i in range(4)]
    for c in copies:
        c.start()
    for c in copies:
        c.wait()


def shards(user_emb, item_emb, user_cot, item_cot, tiles, tile_cols, row_count, user_deg, item_deg):
    out = jax.ShapeDtypeStruct((SHARD, WIDTH), F32)
    dma = pltpu.SemaphoreType.DMA
    square = (SHARD, WIDTH)
    piece = (HALF, WIDTH)
    results = pl.pallas_call(
        layer_kernel,
        name="layer",
        out_shape=(pltpu.VMEM((SHARD, WIDTH), F32),) * 4,
        in_specs=[ANY] * 9,
        out_specs=(VM,) * 4,
        scratch_shapes=[
            pltpu.VMEM((SLOTS + 1, USERS, BLOCK), BF16),
            pltpu.VMEM((USERS, ITEMS), BF16),
            pltpu.VMEM((2, USERS, WIDTH), BF16),
            pltpu.VMEM((2, ITEMS, WIDTH), BF16),
            pltpu.VMEM((4,) + square, BF16),
            pltpu.VMEM((2, 2, BLOCK), jnp.int32),
            pltpu.VMEM((SLOTS, ROWS), jnp.int32),
            pltpu.VMEM((1, ROWS), jnp.int32),
            pltpu.VMEM((COLS, ROWS), jnp.int32),
            pltpu.SMEM((COLS, ROWS), jnp.int32),
            pltpu.VMEM((2, SHARD, BLOCK), F32),
            pltpu.VMEM((STEPS,) + square, F32),
            pltpu.VMEM((STEPS,) + square, F32),
            pltpu.VMEM((STEPS,) + square, BF16),
            pltpu.VMEM((STEPS,) + square, BF16),
            pltpu.VMEM((STEPS,) + square, BF16),
            pltpu.VMEM((2, 2, 2) + piece, BF16),
            pltpu.VMEM((2, 2, 2) + square, BF16),
            pltpu.VMEM((2,) + square, BF16),
            pltpu.VMEM((2,) + square, BF16),
            pltpu.VMEM((STEPS,) + square, BF16),
            pltpu.VMEM((2, 2, 2) + piece, BF16),
            pltpu.VMEM((2, 2, 2) + square, BF16),
            pltpu.VMEM((2,) + square, BF16),
            pltpu.VMEM((2,) + square, BF16),
            dma((8,)), dma((SLOTS,)), dma, dma((4, 2)),
            dma((2, 32)), dma((2, 16)), dma((16,)), dma((2, 4)), dma((2, 8)), dma((2, 2)),
            dma((2, 4)), dma((2, 8)), dma((2, 2)),
        ],
        compiler_params=pltpu.CompilerParams(
            collective_id=0, has_side_effects=True, vmem_limit_bytes=62 << 20),
    )(user_emb, item_emb, user_cot, item_cot, tiles, tile_cols.T, row_count.T,
      user_deg.reshape(2, BLOCK), item_deg.reshape(2, BLOCK))
    return pl.pallas_call(
        store_kernel,
        name="store",
        out_shape=(out,) * 4,
        in_specs=[ANY] * 4,
        compiler_params=pltpu.CompilerParams(vmem_limit_bytes=1 << 20),
        out_specs=(ANY,) * 4,
        scratch_shapes=[dma((4,))],
    )(*results)


def solution(mesh):
    nodes = P(("row", "col"), None)
    in_specs = (nodes, nodes, nodes, nodes, P("row", "col"), P("row", "col"), P("row", "col"),
                P(("row", "col")), P(("row", "col")))
    return jax.shard_map(shards, mesh=mesh, in_specs=in_specs, out_specs=(nodes,) * 4, check_vma=False)
```
